32 devices in a mesh: row: 8 (over y, x, core), col: 4 (over z).
Axes of the slice: x: 2, y: 2, z: 4, core: 2. Of those that a mesh axis runs over, the one named last changes fastest.
Arguments:
- matrix: float32 [16, 8, 128, 32, 4, 128], P(None, 'row', None, None, 'col'), may hold values from -6 to 6
- reflectors: float32 [32, 4, 128, 512], P(None, 'col'), as said below
Outputs:
- updated: float32 [16, 8, 128, 32, 4, 128], P(None, 'row', None, None, 'col')
The draws below stay inside these ranges and needn't reach their ends.
Inputs may be any that keep to these rules, and one draw needn't show every extreme that they name: Read as a 16384 x 512 matrix, the columns of reflectors are orthonormal.
All inputs are finite; a program needn't handle non-finite values.
Results may differ from the reference program's by a relative error of at most 0.0001.
Values sent between devices are 32-bit elements; how exact they have to be, the bound alone decides.
No kernel may reach another device: no remote copies, remote signals or barrier semaphores. Data moves between devices by JAX's collectives and lax.ppermute only.
A program may use at most 192 MiB of HBM per device.

```python
import jax
import jax.numpy as jnp
from jax import lax

ORDER = 16384
TILE = 128
PANEL = 256
PANELS = 2
RT = 16
CT = 32
N_ROW = 8
N_COL = 4


def draw_reflectors(key, part):
    first_key = jax.random.fold_in(key, 11)
    source = jax.random.normal(first_key, (ORDER, PANEL * PANELS), jnp.float32)
    orthonormal, _ = jnp.linalg.qr(source)
    return orthonormal.reshape(CT, ORDER // (CT * TILE), TILE, PANEL * PANELS).astype(jnp.float32)


def level_of(own_key, dims, pieces, low, largest):
    def one(dim, shards_of):
        heights = jax.random.uniform(jax.random.fold_in(jax.random.fold_in(own_key, 6), dim), (shards_of,), jnp.float32, low / len(pieces), largest / len(pieces))
        return jnp.repeat(jnp.exp(heights), dims[dim] // shards_of).reshape((-1,) + (1,) * (len(dims) - dim - 1))

    factor_of = one(*pieces[0])
    for cut in pieces[1:]:
        factor_of = factor_of * one(*cut)
    return factor_of


def bell_draw(stream_key, shape, width, most, pieces=(), dtype=jnp.bfloat16):
    result = jax.random.normal(stream_key, shape, jnp.float32) * width
    if len(pieces) > 0:
        result = level_of(stream_key, shape, pieces, -0.22, 0.18) * result
    return jnp.clip(result, min=-most, max=most).astype(dtype)


def setup_inputs(seed: int = 0) -> dict:
    key_list = jax.random.split(jax.random.key(seed), 3)
    matrix = bell_draw(key_list[0], (RT, N_ROW, TILE, CT, N_COL, TILE), 1.0, 6.0, ((1, 8), (4, 4)), jnp.float32)
    reflectors = draw_reflectors(jax.random.fold_in(key_list[2], 71), 0)
    return dict(matrix=matrix, reflectors=reflectors)


def reference(matrix, reflectors):
    stored = matrix.reshape(ORDER, ORDER)
    current = jnp.tril(stored) + jnp.tril(stored, -1).T
    basis = reflectors.reshape(ORDER, PANEL * PANELS)
    for panel in range(PANELS):
        vectors = basis[:, panel * PANEL:(panel + 1) * PANEL]
        product = jnp.dot(current.astype(jnp.float32), vectors.astype(jnp.float32), precision=lax.Precision.HIGHEST, preferred_element_type=jnp.float32)
        projection = jnp.dot(vectors.T.astype(jnp.float32), product.astype(jnp.float32), precision=lax.Precision.HIGHEST, preferred_element_type=jnp.float32)
        product = product - 0.5 * jnp.dot(vectors.astype(jnp.float32), projection.astype(jnp.float32), precision=lax.Precision.HIGHEST, preferred_element_type=jnp.float32)
        left_side = jnp.concatenate([vectors, product], axis=1)
        right_side = jnp.concatenate([product, vectors], axis=1)
        current = current - jnp.dot(left_side.astype(jnp.float32), right_side.T.astype(jnp.float32), precision=lax.Precision.HIGHEST, preferred_element_type=jnp.float32)
    return jnp.tril(current).reshape(matrix.shape)
```

```python
import functools

import jax
import jax.numpy as jnp
import numpy as np
from jax import lax
from jax.experimental import pallas as pl
from jax.experimental.pallas import tpu as pltpu
from jax.sharding import PartitionSpec as P

F32 = jnp.float32
BF16 = jnp.bfloat16
BLOCK_TILES = 4
PANELS = 2


def split(x):
    high = x.astype(BF16)
    return high, (x - high.astype(F32)).astype(BF16)


def dot1(a, b, ca, cb):
    return lax.dot_general(a, b, (((ca,), (cb,)), ((), ())), preferred_element_type=F32)


def dot3(a, b, ca, cb):
    return dot1(a[0], b[0], ca, cb) + dot1(a[0], b[1], ca, cb) + dot1(a[1], b[0], ca, cb)


class Plan:
    def __init__(self, row_tiles, tile, col_tiles, row_count, col_count):
        self.tile, self.row_tiles, self.col_tiles = tile, row_tiles, col_tiles
        self.row_count, self.col_count = row_count, col_count
        self.stride = row_count // col_count
        self.br = BLOCK_TILES
        self.bc = BLOCK_TILES * self.stride
        self.blocks = row_tiles // self.br
        self.rows, self.cols = self.br * tile, self.bc * tile

    def ids(self, shape, a, b, place):
        r = lax.broadcasted_iota(jnp.int32, shape, 0) + a * self.rows
        c = lax.broadcasted_iota(jnp.int32, shape, 1) + b * self.cols
        t = self.tile
        gr = ((r // t) * self.row_count + place[0]) * t + r % t
        gc = ((c // t) * self.col_count + place[1]) * t + c % t
        return gr, gc

    def load(self, ref):
        return jnp.concatenate([ref[:, m, :] for m in range(self.bc)], axis=1)

    def half_lower(self, ref, a, b, place):
        x = self.load(ref)
        gr, gc = self.ids(x.shape, a, b, place)
        return jnp.where(gr > gc, x, jnp.where(gr == gc, 0.5 * x, 0.0))

    def tables(self, pairs):
        return tuple(jnp.asarray(np.array([p[n] for p in pairs], np.int32)) for n in (0, 1))

    def a_spec(self, index):
        return pl.BlockSpec((self.rows, self.bc, self.tile), index)

    def params(self):
        return pltpu.CompilerParams(vmem_limit_bytes=60 << 20)


def first_kernel(plan, at, bt, place, a_ref, v_ref, o0_ref, o1_ref, h_ref, l_ref, vh, vl):
    g = pl.program_id(0)
    a, b = at[g], bt[g]

    @pl.when(g == 0)
    def _():
        vh[...], vl[...] = split(v_ref[...])

    x = split(plan.half_lower(a_ref, a, b, place))
    h_ref[...], l_ref[...] = x
    s = pl.ds(pl.multiple_of(b * plan.cols, plan.cols), plan.cols)
    d = dot3(x, (vh[s, :], vl[s, :]), 1, 0)
    w = o0_ref.shape[1]

    @pl.when(b == 0)
    def _():
        o0_ref[...] = d[:, :w]
        o1_ref[...] = d[:, w:]

    @pl.when(b > 0)
    def _():
        o0_ref[...] += d[:, :w]
        o1_ref[...] += d[:, w:]


def whole(x):
    return pl.BlockSpec(x.shape, lambda g, *_: (0, 0), pipeline_mode=pl.Buffered(1))


def cost(plan, n, passes=3):
    area = plan.rows * plan.cols * (plan.blocks * (plan.blocks + 1) // 2)
    return pl.CostEstimate(flops=2 * passes * area * n, bytes_accessed=4 * area, transcendentals=0)


def direct_first(plan, a, v, place):
    at, bt = plan.tables([(i, j) for i in range(plan.blocks) for j in range(i + 1)])
    n = v.shape[1]
    block = pl.BlockSpec((plan.rows, plan.cols), lambda g, at, bt, p: (at[g], bt[g]))
    flat = jax.ShapeDtypeStruct((a.shape[0], a.shape[1] * a.shape[2]), BF16)
    return pl.pallas_call(
        functools.partial(first_kernel, plan),
        grid_spec=pltpu.PrefetchScalarGridSpec(
            num_scalar_prefetch=3,
            grid=(at.shape[0],),
            in_specs=[plan.a_spec(lambda g, at, bt, p: (at[g], bt[g], 0)), whole(v)],
            out_specs=[pl.BlockSpec((plan.rows, n // 2), lambda g, at, bt, p: (at[g], 0))] * 2 + [block, block],
            scratch_shapes=[pltpu.VMEM(v.shape, BF16)] * 2,
        ),
        out_shape=[jax.ShapeDtypeStruct((a.shape[0], n // 2), F32)] * 2 + [flat, flat],
        cost_estimate=cost(plan, n),
        compiler_params=plan.params(),
        name="direct_first",
    )(at, bt, place, a, v)


def trans_kernel(plan, at, bt, h_ref, l_ref, v_ref, o_ref, vh, vl):
    g = pl.program_id(0)
    a, b = at[g], bt[g]

    @pl.when(g == 0)
    def _():
        vh[...], vl[...] = split(v_ref[...])

    s = pl.ds(pl.multiple_of(a * plan.rows, plan.rows), plan.rows)
    d = dot3((h_ref[...], l_ref[...]), (vh[s, :], vl[s, :]), 0, 0)

    @pl.when(a == b)
    def _():
        o_ref[...] = d

    @pl.when(a > b)
    def _():
        o_ref[...] += d


def trans(plan, h, l, v):
    at, bt = plan.tables([(i, j) for j in range(plan.blocks) for i in range(j, plan.blocks)])
    n = v.shape[1]
    block = pl.BlockSpec((plan.rows, plan.cols), lambda g, at, bt: (at[g], bt[g]))
    return pl.pallas_call(
        functools.partial(trans_kernel, plan),
        grid_spec=pltpu.PrefetchScalarGridSpec(
            num_scalar_prefetch=2,
            grid=(at.shape[0],),
            in_specs=[block, block, whole(v)],
            out_specs=pl.BlockSpec((plan.cols, n), lambda g, at, bt: (bt[g], 0)),
            scratch_shapes=[pltpu.VMEM(v.shape, BF16)] * 2,
        ),
        out_shape=jax.ShapeDtypeStruct((h.shape[1], n), F32),
        cost_estimate=cost(plan, n),
        compiler_params=plan.params(),
        name="trans",
    )(at, bt, h, l, v)


def near_kernel(plan, panels, at, bt, *refs):
    a_ref, vr = refs[0], refs[1 : 1 + panels]
    yc = refs[1 + panels : 1 + 2 * panels]
    o_ref, vrh, vrl, ych, ycl = refs[1 + 2 * panels :]
    g = pl.program_id(0)
    a, b = at[g], bt[g]
    w = ych.shape[1] // panels

    @pl.when(g == 0)
    def _():
        for p in range(panels):
            vrh[:, p * w : (p + 1) * w], vrl[:, p * w : (p + 1) * w] = split(vr[p][...])

    @pl.when(a == b)
    def _():
        for p in range(panels):
            ych[:, p * w : (p + 1) * w], ycl[:, p * w : (p + 1) * w] = split(yc[p][...])

    s = pl.ds(pl.multiple_of(a * plan.rows, plan.rows), plan.rows)
    o_ref[...] = plan.load(a_ref) - dot3((vrh[s, :], vrl[s, :]), (ych[...], ycl[...]), 1, 1)


def near(plan, a, vr, yc):
    at, bt = plan.tables([(i, j) for j in range(plan.blocks) for i in range(j, plan.blocks)])
    w = vr[0].shape[1]
    n = w * len(vr)
    strip = lambda q: pl.BlockSpec((plan.cols, w), lambda g, at, bt: (bt[g], q))
    return pl.pallas_call(
        functools.partial(near_kernel, plan, len(yc)),
        grid_spec=pltpu.PrefetchScalarGridSpec(
            num_scalar_prefetch=2,
            grid=(at.shape[0],),
            in_specs=[plan.a_spec(lambda g, at, bt: (at[g], bt[g], 0))] + [whole(v) for v in vr] + [strip(q) for _, q in yc],
            out_specs=pl.BlockSpec((plan.rows, plan.cols), lambda g, at, bt: (at[g], bt[g])),
            scratch_shapes=[pltpu.VMEM((a.shape[0], n), BF16)] * 2 + [pltpu.VMEM((plan.cols, n), BF16)] * 2,
        ),
        out_shape=jax.ShapeDtypeStruct((a.shape[0], a.shape[1] * a.shape[2]), F32),
        cost_estimate=cost(plan, n),
        compiler_params=plan.params(),
        name="near",
    )(at, bt, a, *vr, *[y for y, _ in yc])


def far_kernel(plan, at, bt, place, x_ref, y_ref, v_ref, o_ref, yh, yl, vh, vl):
    g = pl.program_id(0)
    a, b = at[g], bt[g]

    @pl.when(g == 0)
    def _():
        yh[...], yl[...] = split(y_ref[...])

    @pl.when(a == b)
    def _():
        vh[...], vl[...] = split(v_ref[...])

    @pl.when(b > a)
    def _():
        o_ref[...] = jnp.zeros(o_ref.shape, F32)

    @pl.when(b <= a)
    def _():
        s = pl.ds(pl.multiple_of(a * plan.rows, plan.rows), plan.rows)
        x = x_ref[...] - dot3((yh[s, :], yl[s, :]), (vh[...], vl[...]), 1, 1)
        gr, gc = plan.ids(x.shape, a, b, place)
        x = jnp.where(gr >= gc, x, 0.0)
        for m in range(plan.bc):
            o_ref[:, m, :] = x[:, m * plan.tile : (m + 1) * plan.tile]


def far(plan, x, y, v, q, place):
    at, bt = plan.tables([(i, j) for j in range(plan.blocks) for i in range(plan.blocks)])
    n = y.shape[1]
    return pl.pallas_call(
        functools.partial(far_kernel, plan),
        grid_spec=pltpu.PrefetchScalarGridSpec(
            num_scalar_prefetch=3,
            grid=(at.shape[0],),
            in_specs=[
                pl.BlockSpec((plan.rows, plan.cols), lambda g, at, bt, p: (jnp.maximum(at[g], bt[g]), bt[g])),
                whole(y),
                pl.BlockSpec((plan.cols, n), lambda g, at, bt, p: (bt[g], q)),
            ],
            out_specs=plan.a_spec(lambda g, at, bt, p: (at[g], bt[g], 0)),
            scratch_shapes=[pltpu.VMEM(y.shape, BF16)] * 2 + [pltpu.VMEM((plan.cols, n), BF16)] * 2,
        ),
        out_shape=jax.ShapeDtypeStruct((x.shape[0], x.shape[1] // plan.tile, plan.tile), F32),
        cost_estimate=cost(plan, n),
        compiler_params=plan.params(),
        name="far",
    )(at, bt, place, x, y, v)


def high(a, b, ca, cb):
    return lax.dot_general(
        a, b, (((ca,), (cb,)), ((), ())), precision=lax.Precision.HIGH, preferred_element_type=F32
    )


def body(matrix, reflectors):
    row_count, col_count = lax.axis_size("row"), lax.axis_size("col")
    row, col = lax.axis_index("row"), lax.axis_index("col")
    row_tiles, _, tile, col_tiles, _, _ = matrix.shape
    rank = reflectors.shape[3]
    plan = Plan(row_tiles, tile, col_tiles, row_count, col_count)
    stride = plan.stride
    rows, cols = row_tiles * tile, col_tiles * tile
    a = matrix.reshape(rows, col_tiles, tile)
    place = jnp.stack([row, col]).astype(jnp.int32)
    both = ("row", "col")
    part = row // col_count
    gap = jnp.bitwise_xor(row % col_count, col)
    bits = [1 << n for n in range(col_count.bit_length() - 1)]
    vc = reflectors.reshape(cols, rank)
    width = rank // PANELS

    def own_rows(x):
        blocks = x.reshape(row_tiles, stride, tile, x.shape[1])
        return lax.dynamic_index_in_dim(blocks, part, axis=1, keepdims=False).reshape(rows, x.shape[1])

    def pairs(keep, bit):
        out = []
        for i in range(row_count):
            for z in range(col_count):
                if keep((i % col_count) ^ z):
                    out.append((i * col_count + z, i * col_count + (z ^ bit)))
        return out

    def tie(x, *after):
        return lax.optimization_barrier((x, *after))[0]

    def hop_out(x, bit):
        done = sum(n for n in bits if n > bit)
        return lax.ppermute(x, both, pairs(lambda code: code & ~done == 0, bit))

    def take(x, got, bit):
        mine = (jnp.bitwise_and(gap, bit) != 0) & (jnp.bitwise_and(gap, bit - 1) == 0)
        return jnp.where(mine, got, x)

    def mid_out(x):
        for bit in reversed(bits[1:-1]):
            x = take(x, hop_out(x, bit), bit)
        return x

    def mid_in(x):
        for bit in bits[1:-1]:
            x = x + hop_in(x, bit)
        return x

    def hop_in(x, bit):
        return lax.ppermute(x, both, pairs(lambda code: code & bit and code & (bit - 1) == 0, bit))

    def swap(x, axis, count, bit):
        return lax.ppermute(x, axis, [(n, n ^ bit) for n in range(count)])

    def halves(x, bit):
        x = x.reshape(2, x.shape[0] // 2, *x.shape[1:])
        mine = (jnp.bitwise_and(row, bit) != 0).astype(jnp.int32)
        keep = lax.dynamic_index_in_dim(x, mine, 0, keepdims=False)
        send = lax.dynamic_index_in_dim(x, 1 - mine, 0, keepdims=False)
        return keep, send

    def joined(x, got, bit):
        upper = jnp.bitwise_and(row, bit) != 0
        return jnp.concatenate([jnp.where(upper, got, x), jnp.where(upper, x, got)], axis=0)

    def collect(x, order):
        for bit in reversed(order):
            x = joined(x, swap(x, "row", row_count, bit), bit)
        return x

    row_bits = [1 << n for n in range(row_count.bit_length() - 1)]
    others = row_count // 2
    chip = row // 2

    def cross(x, code):
        return lax.ppermute(x, "row", [(n, n ^ (2 * code)) for n in range(row_count)])

    def sum_steps(x):
        keep, send = halves(x, 1)
        got = swap(send, "row", row_count, 1)
        prev = yield
        x = tie(keep, prev) + got
        x = x.reshape(others, x.shape[0] // others, x.shape[1])
        pick = lambda code: lax.dynamic_index_in_dim(x, jnp.bitwise_xor(chip, code), 0, keepdims=False)
        got = [cross(pick(code), code) for code in range(1, others)]
        prev = yield x
        piece = tie(pick(0), prev)
        for g in got:
            piece = piece + g
        got = [cross(piece, code) for code in range(1, others)]
        prev = yield piece
        stack = [tie(piece, prev)] + got
        bit = 1
        while bit < others:
            flip = jnp.bitwise_and(chip, bit) != 0
            stack = [jnp.where(flip, stack[n ^ bit], stack[n]) for n in range(others)]
            bit *= 2
        x = jnp.concatenate(stack, axis=0)
        got = swap(x, "row", row_count, 1)
        prev = yield x
        yield joined(tie(x, prev), got, 1)

    own = own_rows(vc)
    own = lax.optimization_barrier([own[:, p * width : (p + 1) * width] for p in range(PANELS)])

    def with_direct(t, dp):
        t = t.reshape(row_tiles, stride, tile, width)
        here = (jnp.arange(stride) == part)[None, :, None, None] & (gap == 0)
        t = t + jnp.where(here, dp.reshape(row_tiles, 1, tile, width), 0.0)
        return t.reshape(cols, width)

    ga0 = hop_out(own[0], bits[-1])
    d0, d1, high_part, low_part = direct_first(plan, a, vc, place)
    b0 = hop_in(d0, bits[0])
    x0 = mid_out(take(own[0], tie(ga0, d1), bits[-1]))
    gb0 = hop_out(x0, bits[0])
    d0 = mid_in(tie(d0, x0) + b0)
    a0 = hop_in(d0, bits[-1])
    ga1 = hop_out(tie(own[1], d0), bits[-1])
    v0 = take(tie(x0, d0), gb0, bits[0])
    t0 = trans(plan, high_part, low_part, v0)
    t0 = with_direct(t0, tie(d0, t0) + a0)
    s0 = sum_steps(t0)
    next(s0)
    x1 = mid_out(take(tie(own[1], t0), ga1, bits[-1]))
    gb1 = hop_out(x1, bits[0])
    b1 = hop_in(tie(d1, x1), bits[0])
    e = s0.send(x1)
    d1 = mid_in(tie(d1, e) + b1)
    a1 = hop_in(d1, bits[-1])
    v1 = take(tie(x1, d1), gb1, bits[0])
    t1 = trans(plan, high_part, low_part, v1)
    e = s0.send(t1)
    e = s0.send(e)
    d1 = tie(d1, e) + a1
    s1 = sum_steps(with_direct(t1, d1))
    next(s1)
    e = d1
    y0 = s0.send(e)
    e = s1.send(y0)
    oy0 = own_rows(y0)
    ga0 = hop_out(oy0, bits[-1])
    e = s1.send(oy0)
    x0 = mid_out(take(tie(oy0, e), ga0, bits[-1]))
    gb0 = hop_out(x0, bits[0])
    e = s1.send(x0)
    y1 = s1.send(e)
    oy1 = own_rows(y1)
    ga1 = hop_out(oy1, bits[-1])
    piece = rank // row_count
    mine = lax.dynamic_slice_in_dim(vc, row * piece, piece, axis=1)
    m = [high(tie(mine, oy1), y, 0, 0) for y in (y0, y1)]
    m = jnp.concatenate(m, axis=1)
    got = swap(m, "col", col_count, bits[-1])
    x = near(plan, a, [v0, v1], [(tie(y0, m), 0), (y1, 0)])
    m = tie(m, x) + got
    for bit in reversed(bits[:-1]):
        m = m + swap(m, "col", col_count, bit)
    x1 = mid_out(take(tie(oy1, m), ga1, bits[-1]))
    gb1 = hop_out(x1, bits[0])
    m = collect(tie(m, x1), row_bits[::-1])
    fix = high(jnp.concatenate([v0, v1], axis=1), m, 1, 0)
    r0 = take(tie(x0, fix), gb0, bits[0])
    r1 = take(tie(x1, r0), gb1, bits[0])
    yr = jnp.concatenate([r0, r1], axis=1) - fix
    return far(plan, x, yr, vc, 0, place).reshape(matrix.shape)


def solution(mesh):
    placed = (P(None, "row", None, None, "col", None), P(None, "col", None, None))
    return jax.shard_map(
        body,
        mesh=mesh,
        in_specs=placed,
        out_specs=P(None, "row", None, None, "col", None),
        check_vma=False,
    )
```

```python
import functools

import jax
import jax.numpy as jnp
import numpy as np
from jax import lax
from jax.experimental import pallas as pl
from jax.experimental.pallas import tpu as pltpu
from jax.sharding import PartitionSpec as P

F32 = jnp.float32
BF16 = jnp.bfloat16
BLOCK_TILES = 4
PANELS = 2


def split(x):
    high = x.astype(BF16)
    return high, (x - high.astype(F32)).astype(BF16)


def dot1(a, b, ca, cb):
    return lax.dot_general(a, b, (((ca,), (cb,)), ((), ())), preferred_element_type=F32)


def dot3(a, b, ca, cb):
    return dot1(a[0], b[0], ca, cb) + dot1(a[0], b[1], ca, cb) + dot1(a[1], b[0], ca, cb)


class Plan:
    def __init__(self, row_tiles, tile, col_tiles, row_count, col_count):
        self.tile, self.row_tiles, self.col_tiles = tile, row_tiles, col_tiles
        self.row_count, self.col_count = row_count, col_count
        self.stride = row_count // col_count
        self.br = BLOCK_TILES
        self.bc = BLOCK_TILES * self.stride
        self.blocks = row_tiles // self.br
        self.rows, self.cols = self.br * tile, self.bc * tile

    def ids(self, shape, a, b, place):
        r = lax.broadcasted_iota(jnp.int32, shape, 0) + a * self.rows
        c = lax.broadcasted_iota(jnp.int32, shape, 1) + b * self.cols
        t = self.tile
        gr = ((r // t) * self.row_count + place[0]) * t + r % t
        gc = ((c // t) * self.col_count + place[1]) * t + c % t
        return gr, gc

    def load(self, ref):
        return jnp.concatenate([ref[:, m, :] for m in range(self.bc)], axis=1)

    def half_lower(self, ref, a, b, place):
        x = self.load(ref)
        gr, gc = self.ids(x.shape, a, b, place)
        return jnp.where(gr > gc, x, jnp.where(gr == gc, 0.5 * x, 0.0))

    def tables(self, pairs):
        return tuple(jnp.asarray(np.array([p[n] for p in pairs], np.int32)) for n in (0, 1))

    def a_spec(self, index):
        return pl.BlockSpec((self.rows, self.bc, self.tile), index)

    def params(self):
        return pltpu.CompilerParams(vmem_limit_bytes=60 << 20)


def first_kernel(plan, at, bt, place, a_ref, v_ref, o_ref, h_ref, l_ref, vh, vl):
    g = pl.program_id(0)
    a, b = at[g], bt[g]

    @pl.when(g == 0)
    def _():
        vh[...], vl[...] = split(v_ref[...])

    x = split(plan.half_lower(a_ref, a, b, place))
    h_ref[...], l_ref[...] = x
    s = pl.ds(pl.multiple_of(b * plan.cols, plan.cols), plan.cols)
    d = dot3(x, (vh[s, :], vl[s, :]), 1, 0)

    @pl.when(b == 0)
    def _():
        o_ref[...] = d

    @pl.when(b > 0)
    def _():
        o_ref[...] += d


def direct_kernel(plan, at, bt, h_ref, l_ref, v_ref, o_ref, vh, vl):
    g = pl.program_id(0)
    b = bt[g]

    @pl.when(g == 0)
    def _():
        vh[...], vl[...] = split(v_ref[...])

    s = pl.ds(pl.multiple_of(b * plan.cols, plan.cols), plan.cols)
    d = dot3((h_ref[...], l_ref[...]), (vh[s, :], vl[s, :]), 1, 0)

    @pl.when(b == 0)
    def _():
        o_ref[...] = d

    @pl.when(b > 0)
    def _():
        o_ref[...] += d


def whole(x):
    return pl.BlockSpec(x.shape, lambda g, *_: (0, 0), pipeline_mode=pl.Buffered(1))


def cost(plan, n, passes=3):
    area = plan.rows * plan.cols * (plan.blocks * (plan.blocks + 1) // 2)
    return pl.CostEstimate(flops=2 * passes * area * n, bytes_accessed=4 * area, transcendentals=0)


def strip(x, q, n):
    return pl.BlockSpec((x.shape[0], n), lambda g, *_: (0, q), pipeline_mode=pl.Buffered(1))


def direct_first(plan, a, v, q, width, place):
    at, bt = plan.tables([(i, j) for i in range(plan.blocks) for j in range(i + 1)])
    n = width
    block = pl.BlockSpec((plan.rows, plan.cols), lambda g, at, bt, p: (at[g], bt[g]))
    flat = jax.ShapeDtypeStruct((a.shape[0], a.shape[1] * a.shape[2]), BF16)
    return pl.pallas_call(
        functools.partial(first_kernel, plan),
        grid_spec=pltpu.PrefetchScalarGridSpec(
            num_scalar_prefetch=3,
            grid=(at.shape[0],),
            in_specs=[plan.a_spec(lambda g, at, bt, p: (at[g], bt[g], 0)), strip(v, q, n)],
            out_specs=[pl.BlockSpec((plan.rows, n), lambda g, at, bt, p: (at[g], 0)), block, block],
            scratch_shapes=[pltpu.VMEM((v.shape[0], n), BF16)] * 2,
        ),
        out_shape=[jax.ShapeDtypeStruct((a.shape[0], n), F32), flat, flat],
        cost_estimate=cost(plan, n),
        compiler_params=plan.params(),
        name="direct_first",
    )(at, bt, place, a, v)


def direct(plan, h, l, v, q, width):
    at, bt = plan.tables([(i, j) for i in range(plan.blocks) for j in range(i + 1)])
    n = width
    block = pl.BlockSpec((plan.rows, plan.cols), lambda g, at, bt: (at[g], bt[g]))
    return pl.pallas_call(
        functools.partial(direct_kernel, plan),
        grid_spec=pltpu.PrefetchScalarGridSpec(
            num_scalar_prefetch=2,
            grid=(at.shape[0],),
            in_specs=[block, block, strip(v, q, n)],
            out_specs=pl.BlockSpec((plan.rows, n), lambda g, at, bt: (at[g], 0)),
            scratch_shapes=[pltpu.VMEM((v.shape[0], n), BF16)] * 2,
        ),
        out_shape=jax.ShapeDtypeStruct((h.shape[0], n), F32),
        cost_estimate=cost(plan, n),
        compiler_params=plan.params(),
        name="direct",
    )(at, bt, h, l, v)


def trans_kernel(plan, at, bt, h_ref, l_ref, v_ref, o_ref, vh, vl):
    g = pl.program_id(0)
    a, b = at[g], bt[g]

    @pl.when(g == 0)
    def _():
        vh[...], vl[...] = split(v_ref[...])

    s = pl.ds(pl.multiple_of(a * plan.rows, plan.rows), plan.rows)
    d = dot3((h_ref[...], l_ref[...]), (vh[s, :], vl[s, :]), 0, 0)

    @pl.when(a == b)
    def _():
        o_ref[...] = d

    @pl.when(a > b)
    def _():
        o_ref[...] += d


def trans(plan, h, l, v):
    at, bt = plan.tables([(i, j) for j in range(plan.blocks) for i in range(j, plan.blocks)])
    n = v.shape[1]
    block = pl.BlockSpec((plan.rows, plan.cols), lambda g, at, bt: (at[g], bt[g]))
    return pl.pallas_call(
        functools.partial(trans_kernel, plan),
        grid_spec=pltpu.PrefetchScalarGridSpec(
            num_scalar_prefetch=2,
            grid=(at.shape[0],),
            in_specs=[block, block, whole(v)],
            out_specs=pl.BlockSpec((plan.cols, n), lambda g, at, bt: (bt[g], 0)),
            scratch_shapes=[pltpu.VMEM(v.shape, BF16)] * 2,
        ),
        out_shape=jax.ShapeDtypeStruct((h.shape[1], n), F32),
        cost_estimate=cost(plan, n),
        compiler_params=plan.params(),
        name="trans",
    )(at, bt, h, l, v)


def near_kernel(plan, panels, at, bt, *refs):
    a_ref, vr = refs[0], refs[1 : 1 + panels]
    yc = refs[1 + panels : 1 + 2 * panels]
    o_ref, vrh, vrl, ych, ycl = refs[1 + 2 * panels :]
    g = pl.program_id(0)
    a, b = at[g], bt[g]
    w = ych.shape[1] // panels

    @pl.when(g == 0)
    def _():
        for p in range(panels):
            vrh[:, p * w : (p + 1) * w], vrl[:, p * w : (p + 1) * w] = split(vr[p][...])

    @pl.when(a == b)
    def _():
        for p in range(panels):
            ych[:, p * w : (p + 1) * w], ycl[:, p * w : (p + 1) * w] = split(yc[p][...])

    s = pl.ds(pl.multiple_of(a * plan.rows, plan.rows), plan.rows)
    o_ref[...] = plan.load(a_ref) - dot3((vrh[s, :], vrl[s, :]), (ych[...], ycl[...]), 1, 1)


def near(plan, a, vr, yc):
    at, bt = plan.tables([(i, j) for j in range(plan.blocks) for i in range(j, plan.blocks)])
    w = vr[0].shape[1]
    n = w * len(vr)
    strip = lambda q: pl.BlockSpec((plan.cols, w), lambda g, at, bt: (bt[g], q))
    return pl.pallas_call(
        functools.partial(near_kernel, plan, len(yc)),
        grid_spec=pltpu.PrefetchScalarGridSpec(
            num_scalar_prefetch=2,
            grid=(at.shape[0],),
            in_specs=[plan.a_spec(lambda g, at, bt: (at[g], bt[g], 0))] + [whole(v) for v in vr] + [strip(q) for _, q in yc],
            out_specs=pl.BlockSpec((plan.rows, plan.cols), lambda g, at, bt: (at[g], bt[g])),
            scratch_shapes=[pltpu.VMEM((a.shape[0], n), BF16)] * 2 + [pltpu.VMEM((plan.cols, n), BF16)] * 2,
        ),
        out_shape=jax.ShapeDtypeStruct((a.shape[0], a.shape[1] * a.shape[2]), F32),
        cost_estimate=cost(plan, n),
        compiler_params=plan.params(),
        name="near",
    )(at, bt, a, *vr, *[y for y, _ in yc])


def far_kernel(plan, at, bt, place, x_ref, y_ref, v_ref, o_ref, yh, yl, vh, vl):
    g = pl.program_id(0)
    a, b = at[g], bt[g]

    @pl.when(g == 0)
    def _():
        yh[...], yl[...] = split(y_ref[...])

    @pl.when(a == b)
    def _():
        vh[...], vl[...] = split(v_ref[...])

    @pl.when(b > a)
    def _():
        o_ref[...] = jnp.zeros(o_ref.shape, F32)

    @pl.when(b <= a)
    def _():
        s = pl.ds(pl.multiple_of(a * plan.rows, plan.rows), plan.rows)
        x = x_ref[...] - dot3((yh[s, :], yl[s, :]), (vh[...], vl[...]), 1, 1)
        gr, gc = plan.ids(x.shape, a, b, place)
        x = jnp.where(gr >= gc, x, 0.0)
        for m in range(plan.bc):
            o_ref[:, m, :] = x[:, m * plan.tile : (m + 1) * plan.tile]


def far(plan, x, y, v, q, place):
    at, bt = plan.tables([(i, j) for j in range(plan.blocks) for i in range(plan.blocks)])
    n = y.shape[1]
    return pl.pallas_call(
        functools.partial(far_kernel, plan),
        grid_spec=pltpu.PrefetchScalarGridSpec(
            num_scalar_prefetch=3,
            grid=(at.shape[0],),
            in_specs=[
                pl.BlockSpec((plan.rows, plan.cols), lambda g, at, bt, p: (jnp.maximum(at[g], bt[g]), bt[g])),
                whole(y),
                pl.BlockSpec((plan.cols, n), lambda g, at, bt, p: (bt[g], q)),
            ],
            out_specs=plan.a_spec(lambda g, at, bt, p: (at[g], bt[g], 0)),
            scratch_shapes=[pltpu.VMEM(y.shape, BF16)] * 2 + [pltpu.VMEM((plan.cols, n), BF16)] * 2,
        ),
        out_shape=jax.ShapeDtypeStruct((x.shape[0], x.shape[1] // plan.tile, plan.tile), F32),
        cost_estimate=cost(plan, n),
        compiler_params=plan.params(),
        name="far",
    )(at, bt, place, x, y, v)


def high(a, b, ca, cb):
    return lax.dot_general(
        a, b, (((ca,), (cb,)), ((), ())), precision=lax.Precision.HIGH, preferred_element_type=F32
    )


def body(matrix, reflectors):
    row_count, col_count = lax.axis_size("row"), lax.axis_size("col")
    row, col = lax.axis_index("row"), lax.axis_index("col")
    row_tiles, _, tile, col_tiles, _, _ = matrix.shape
    rank = reflectors.shape[3]
    plan = Plan(row_tiles, tile, col_tiles, row_count, col_count)
    stride = plan.stride
    rows, cols = row_tiles * tile, col_tiles * tile
    a = matrix.reshape(rows, col_tiles, tile)
    place = jnp.stack([row, col]).astype(jnp.int32)
    both = ("row", "col")
    part = row // col_count
    gap = jnp.bitwise_xor(row % col_count, col)
    bits = [1 << n for n in range(col_count.bit_length() - 1)]
    vc = reflectors.reshape(cols, rank)
    width = rank // PANELS

    def own_rows(x):
        blocks = x.reshape(row_tiles, stride, tile, x.shape[1])
        return lax.dynamic_index_in_dim(blocks, part, axis=1, keepdims=False).reshape(rows, x.shape[1])

    def pairs(keep, bit):
        out = []
        for i in range(row_count):
            for z in range(col_count):
                if keep((i % col_count) ^ z):
                    out.append((i * col_count + z, i * col_count + (z ^ bit)))
        return out

    def tie(x, *after):
        return lax.optimization_barrier((x, *after))[0]

    def hop_out(x, bit):
        done = sum(n for n in bits if n > bit)
        return lax.ppermute(x, both, pairs(lambda code: code & ~done == 0, bit))

    def take(x, got, bit):
        mine = (jnp.bitwise_and(gap, bit) != 0) & (jnp.bitwise_and(gap, bit - 1) == 0)
        return jnp.where(mine, got, x)

    def mid_out(x):
        for bit in reversed(bits[1:-1]):
            x = take(x, hop_out(x, bit), bit)
        return x

    def mid_in(x):
        for bit in bits[1:-1]:
            x = x + hop_in(x, bit)
        return x

    def hop_in(x, bit):
        return lax.ppermute(x, both, pairs(lambda code: code & bit and code & (bit - 1) == 0, bit))

    def swap(x, axis, count, bit):
        return lax.ppermute(x, axis, [(n, n ^ bit) for n in range(count)])

    def halves(x, bit):
        x = x.reshape(2, x.shape[0] // 2, *x.shape[1:])
        mine = (jnp.bitwise_and(row, bit) != 0).astype(jnp.int32)
        keep = lax.dynamic_index_in_dim(x, mine, 0, keepdims=False)
        send = lax.dynamic_index_in_dim(x, 1 - mine, 0, keepdims=False)
        return keep, send

    def joined(x, got, bit):
        upper = jnp.bitwise_and(row, bit) != 0
        return jnp.concatenate([jnp.where(upper, got, x), jnp.where(upper, x, got)], axis=0)

    row_bits = [1 << n for n in range(row_count.bit_length() - 1)]
    others = row_count // 2
    chip = row // 2

    def cross(x, code):
        return lax.ppermute(x, "row", [(n, n ^ (2 * code)) for n in range(row_count)])

    def sum_steps(x):
        keep, send = halves(x, 1)
        got = swap(send, "row", row_count, 1)
        prev = yield
        x = tie(keep, prev) + got
        x = x.reshape(others, x.shape[0] // others, x.shape[1])
        pick = lambda code: lax.dynamic_index_in_dim(x, jnp.bitwise_xor(chip, code), 0, keepdims=False)
        got = [cross(pick(code), code) for code in range(1, others)]
        prev = yield x
        piece = tie(pick(0), prev)
        for g in got:
            piece = piece + g
        got = [cross(piece, code) for code in range(1, others)]
        prev = yield piece
        stack = [tie(piece, prev)] + got
        bit = 1
        while bit < others:
            flip = jnp.bitwise_and(chip, bit) != 0
            stack = [jnp.where(flip, stack[n ^ bit], stack[n]) for n in range(others)]
            bit *= 2
        x = jnp.concatenate(stack, axis=0)
        got = swap(x, "row", row_count, 1)
        prev = yield x
        yield joined(tie(x, prev), got, 1)

    own = own_rows(vc)
    own = lax.optimization_barrier([own[:, p * width : (p + 1) * width] for p in range(PANELS)])

    def with_direct(t, dp):
        t = t.reshape(row_tiles, stride, tile, width)
        here = (jnp.arange(stride) == part)[None, :, None, None] & (gap == 0)
        t = t + jnp.where(here, dp.reshape(row_tiles, 1, tile, width), 0.0)
        return t.reshape(cols, width)

    ga0 = hop_out(own[0], bits[-1])
    d0, high_part, low_part = direct_first(plan, a, vc, 0, width, place)
    b0 = hop_in(d0, bits[0])
    d1 = direct(plan, high_part, low_part, vc, 1, width)
    x0 = mid_out(take(own[0], tie(ga0, d1), bits[-1]))
    gb0 = hop_out(x0, bits[0])
    d0 = mid_in(tie(d0, x0) + b0)
    a0 = hop_in(d0, bits[-1])
    v0 = take(tie(x0, d0), gb0, bits[0])
    ga1 = hop_out(tie(own[1], v0), bits[-1])
    b1 = hop_in(tie(d1, v0), bits[0])
    t0 = trans(plan, high_part, low_part, v0)
    t0 = with_direct(t0, tie(d0, t0) + a0)
    s0 = sum_steps(t0)
    next(s0)
    x1 = mid_out(take(tie(own[1], t0), ga1, bits[-1]))
    gb1 = hop_out(x1, bits[0])
    e = s0.send(x1)
    d1 = mid_in(tie(d1, e) + b1)
    a1 = hop_in(d1, bits[-1])
    v1 = take(tie(x1, d1), gb1, bits[0])
    t1 = trans(plan, high_part, low_part, v1)
    e = s0.send(t1)
    e = s0.send(e)
    d1 = tie(d1, e) + a1
    s1 = sum_steps(with_direct(t1, d1))
    next(s1)
    e = d1
    y0 = s0.send(e)
    e = s1.send(y0)
    oy0 = own_rows(y0)
    ga0 = hop_out(oy0, bits[-1])
    e = s1.send(oy0)
    x0 = mid_out(take(tie(oy0, e), ga0, bits[-1]))
    gb0 = hop_out(x0, bits[0])
    e = s1.send(x0)
    y1 = s1.send(e)
    oy1 = own_rows(y1)
    ga1 = hop_out(oy1, bits[-1])
    piece = rank // row_count
    mine = lax.dynamic_slice_in_dim(vc, row * piece, piece, axis=1)
    m = [high(tie(mine, oy1), y, 0, 0) for y in (y0, y1)]
    m = jnp.concatenate(m, axis=1)
    zs = [lax.ppermute(m, "col", [(n, n ^ c) for n in range(col_count)]) for c in range(1, col_count)]
    x = near(plan, a, [v0, v1], [(tie(y0, m), 0), (y1, 0)])
    m = tie(m, x)
    for g in zs:
        m = m + g
    x1 = mid_out(take(tie(oy1, m), ga1, bits[-1]))
    gb1 = hop_out(x1, bits[0])
    stack = [m] + [lax.ppermute(m, "row", [(n, n ^ c) for n in range(row_count)]) for c in range(1, row_count)]
    for bit in row_bits:
        flip = jnp.bitwise_and(row, bit) != 0
        stack = [jnp.where(flip, stack[n ^ bit], stack[n]) for n in range(row_count)]
    m = jnp.concatenate(stack, axis=0)
    fix = high(jnp.concatenate([v0, v1], axis=1), m, 1, 0)
    r0 = take(tie(x0, fix), gb0, bits[0])
    r1 = take(tie(x1, r0), gb1, bits[0])
    yr = jnp.concatenate([r0, r1], axis=1) - fix
    return far(plan, x, yr, vc, 0, place).reshape(matrix.shape)


def solution(mesh):
    placed = (P(None, "row", None, None, "col", None), P(None, "col", None, None))
    return jax.shard_map(
        body,
        mesh=mesh,
        in_specs=placed,
        out_specs=P(None, "row", None, None, "col", None),
        check_vma=False,
    )
```
